32 devices in a mesh: seq: 8 (over y, x, core), mp: 4 (over z).
Axes of the slice: x: 2, y: 2, z: 4, core: 2. Of those that a mesh axis runs over, the one named last changes fastest.
Arguments:
- queries: bfloat16 [8, 96, 64, 128], P('seq', None, 'mp'), may hold values from -12 to 12
- new_keys: bfloat16 [8, 96, 8, 128], P('seq', None, 'mp'), may hold values from -8 to 8
- new_values: bfloat16 [8, 96, 8, 128], P('seq', None, 'mp'), may hold values from -6 to 6
- pool_keys: bfloat16 [128, 8, 128, 128], P('seq', 'mp'), may hold values from -8 to 8
- pool_values: bfloat16 [128, 8, 128, 128], P('seq', 'mp'), may hold values from -6 to 6
- prefix_len: int32 [8], replicated, may hold values from 1 to 2048, as said below
- page_table: int32 [8, 16], replicated, may hold values from -1 to 127, as said below
- out_weight: bfloat16 [8192, 8192], P('mp'), may hold values from -0.0625 to 0.0625
Outputs:
- attended: bfloat16 [8, 96, 8192], P('seq', None, 'mp')
The draws below stay inside these ranges and needn't reach their ends.
Inputs may be any that keep to these rules, and one draw needn't show every extreme that they name: Prompt r's prefix holds prefix_len[r] tokens in its first ceil(prefix_len[r] / 128) page-table entries. `page_table`: entry [r, l] is the pool page holding positions l * 128 to l * 128 + 127 of prompt r's prefix; entries past the prefix are -1; no pool page appears twice in the table. Pool page p lies on seq index p // 16; one row of the table names at most 2 pages of one seq index, and some row names exactly 2 pages of some seq index.
All inputs are finite; a program needn't handle non-finite values.
Results may differ from the reference program's by a relative error of at most 0.012.
Values may be sent and summed in bfloat16 or wider, within the bound.
A program may use at most 192 MiB of HBM per device.

```python
import jax
import jax.numpy as jnp
from jax import lax

D = 8192
QH = 64
KVH = 8
HD = 128
PAGE = 128
C = 96
R_DEV = 1
P_DEV = 16
REQS = 8
POOL = 128
MAXP = 16
N_SEQ = 8
N_MP = 4


def page_plan(key):
    key = jax.random.fold_in(key, 7)
    key_counts, key_long, key_tail, key_shift = jax.random.split(key, 4)
    hold_most = (MAXP + N_SEQ - 1) // N_SEQ
    others_most = min((POOL - MAXP) // (REQS - 1), MAXP - 1, N_SEQ, (P_DEV - hold_most) // R_DEV)
    counts = jax.random.randint(key_counts, (REQS,), 1, others_most + 1)
    longest = jax.random.randint(key_long, (), 0, REQS)
    is_long = jnp.arange(REQS) == longest
    counts = jnp.where(is_long, MAXP, counts)
    tail_tokens = jax.random.randint(key_tail, (REQS,), 1, PAGE + 1)
    lengths = jnp.where(is_long, MAXP * PAGE, (counts - 1) * PAGE + tail_tokens)
    slot_ids = jnp.arange(MAXP)
    homes = jnp.arange(REQS) // R_DEV
    stride = N_SEQ // 2 - 1
    device_ids = (homes[:, None] + N_SEQ // 2 + slot_ids[None, :] * stride) % N_SEQ
    valid = slot_ids[None, :] < counts[:, None]
    on_device = (device_ids[:, :, None] == jnp.arange(N_SEQ)[None, None, :]) & valid[:, :, None]
    flat = on_device.reshape(REQS * MAXP, N_SEQ).astype(jnp.int32)
    ranks = jnp.cumsum(flat, axis=0) - 1
    rank = jnp.sum(jnp.where(flat > 0, ranks, 0), axis=1).reshape(REQS, MAXP)
    shifts = jax.random.randint(key_shift, (N_SEQ,), 0, P_DEV)
    slots = (rank + shifts[device_ids]) % P_DEV
    table = jnp.where(valid, device_ids * P_DEV + slots, -1)
    return (lengths.astype(jnp.int32), table.astype(jnp.int32))


def draw_prefix_len(key, part):
    return page_plan(key)[0]


def draw_page_table(key, part):
    return page_plan(key)[1]


def attention_plan(key):
    key = jax.random.fold_in(key, 11)
    key_query, key_spread, key_keys = jax.random.split(key, 3)
    base = jax.random.normal(key_query, (REQS, C, QH, HD), jnp.float32)
    spread = jnp.exp(jax.random.uniform(key_spread, (REQS, C, QH, 1), jnp.float32, jnp.log(0.5), jnp.log(4.0)))
    query_draw = jnp.clip(base * spread, -12.0, 12.0)
    key_draw = jnp.clip(jax.random.normal(key_keys, (REQS, C, KVH, HD), jnp.float32), -8.0, 8.0)
    return (query_draw, key_draw)


def draw_queries(key, part):
    return attention_plan(key)[0].astype(jnp.bfloat16)


def draw_new_keys(key, part):
    return attention_plan(key)[1].astype(jnp.bfloat16)


def steps_of(rng, extent, cuts, smallest, top_value):
    gain, own = 1.0, jax.random.fold_in(rng, 6)
    for dim, parts in cuts:
        steps = jnp.exp(jax.random.uniform(jax.random.fold_in(own, dim), (parts,), jnp.float32, smallest / len(cuts), top_value / len(cuts)))
        gain = gain * jnp.repeat(steps, extent[dim] // parts).reshape([-1 if axis == dim else 1 for axis in range(len(extent))])
    return gain


def normal_values(rng, shape, scale, bound, cuts=(), kind=jnp.bfloat16):
    drawn = jax.random.normal(rng, shape, jnp.float32) * scale
    if len(cuts) > 0:
        drawn = steps_of(rng, shape, cuts, -0.22, 0.18) * drawn
    return jnp.clip(drawn, min=-bound, max=bound).astype(kind)


def setup_inputs(seed: int = 0) -> dict:
    arg_keys = jax.random.split(jax.random.key(seed), 9)
    return {
        "queries": draw_queries(jax.random.fold_in(arg_keys[8], 71), 0),
        "new_keys": draw_new_keys(jax.random.fold_in(arg_keys[8], 71), 0),
        "new_values": normal_values(arg_keys[2], (REQS, C, KVH, HD), 1.0, 6.0, ((0, 8), (2, 4))),
        "pool_keys": normal_values(arg_keys[3], (POOL, KVH, PAGE, HD), 1.0, 8.0, ((0, 8), (1, 4))),
        "pool_values": normal_values(arg_keys[4], (POOL, KVH, PAGE, HD), 1.0, 6.0, ((0, 8), (1, 4))),
        "prefix_len": draw_prefix_len(jax.random.fold_in(arg_keys[8], 71), 0),
        "page_table": draw_page_table(jax.random.fold_in(arg_keys[8], 71), 0),
        "out_weight": normal_values(arg_keys[7], (QH * HD, D), (QH * HD) ** -0.5, 0.0625, ((0, 4),)),
    }


def reference(queries, new_keys, new_values, pool_keys, pool_values, prefix_len, page_table, out_weight):
    group_size = QH // KVH
    score_scale = 1.0 / (HD ** 0.5)
    token_ids = jnp.arange(MAXP * PAGE, dtype=jnp.int32)
    positions = jnp.arange(C, dtype=jnp.int32)
    causal = (positions[None, :] <= positions[:, None])[:, None, None, :]

    def one_prompt(inputs):
        query_rows, fresh_keys, fresh_values, length, page_ids = inputs
        safe_pages = jnp.maximum(page_ids, 0)
        keys_prefix = pool_keys[safe_pages].astype(jnp.float32).transpose(1, 0, 2, 3).reshape(KVH, MAXP * PAGE, HD)
        values_prefix = pool_values[safe_pages].astype(jnp.float32).transpose(1, 0, 2, 3).reshape(KVH, MAXP * PAGE, HD)
        seen = (token_ids < length) & jnp.repeat(page_ids >= 0, PAGE)
        seen = seen[None, None, None, :]
        grouped = query_rows.astype(jnp.float32).reshape(C, KVH, group_size, HD)
        prefix_scores = jnp.einsum('cjgd,jkd->cjgk', grouped, keys_prefix) * score_scale
        fresh_scores = jnp.einsum('cjgd,ejd->cjge', grouped, fresh_keys.astype(jnp.float32)) * score_scale
        row_peak = jnp.maximum(jnp.max(jnp.where(seen, prefix_scores, -jnp.inf), axis=-1),
                               jnp.max(jnp.where(causal, fresh_scores, -jnp.inf), axis=-1))
        prefix_weights = jnp.where(seen, jnp.exp(prefix_scores - row_peak[..., None]), 0.0)
        fresh_weights = jnp.where(causal, jnp.exp(fresh_scores - row_peak[..., None]), 0.0)
        weight_sum = jnp.sum(prefix_weights, axis=-1) + jnp.sum(fresh_weights, axis=-1)
        prefix_rounded = lax.optimization_barrier(prefix_weights.astype(jnp.bfloat16)).astype(jnp.float32)
        fresh_rounded = lax.optimization_barrier(fresh_weights.astype(jnp.bfloat16)).astype(jnp.float32)
        weighted = jnp.einsum('cjgk,jkd->cjgd', prefix_rounded, values_prefix)
        weighted = weighted + jnp.einsum('cjge,ejd->cjgd', fresh_rounded, fresh_values.astype(jnp.float32))
        return (weighted / weight_sum[..., None]).astype(jnp.bfloat16).reshape(C, QH * HD)

    attended_heads = lax.map(one_prompt, (queries, new_keys, new_values, prefix_len, page_table))
    flat_heads = attended_heads.reshape(REQS * C, QH * HD)
    group_rows = QH * HD // N_MP
    summed = jnp.zeros((REQS * C, D), jnp.float32)
    for head_group in range(N_MP):
        lower = head_group * group_rows
        partial_value = jnp.dot(flat_heads[:, lower:lower + group_rows], out_weight[lower:lower + group_rows],
                          preferred_element_type=jnp.float32)
        summed = summed + lax.optimization_barrier(partial_value.astype(jnp.bfloat16)).astype(jnp.float32)
    return summed.astype(jnp.bfloat16).reshape(REQS, C, D)
```

```python
import math

import jax
import jax.numpy as jnp
from jax import lax
from jax.sharding import PartitionSpec as P

SLOTS = 2


def on_device(
    queries, new_keys, new_values, pool_keys, pool_values, prefix_len, page_table, out_weight
):
    reqs, fresh, heads, hd = queries.shape
    pages, kvh, page, _ = pool_keys.shape
    rows, maxp = page_table.shape
    group = heads // kvh
    scale = 1.0 / math.sqrt(hd)
    n_seq = lax.axis_size("seq")
    me = lax.axis_index("seq")
    src = jnp.arange(n_seq, dtype=jnp.int32)
    owned = (page_table >= 0)[None] & (page_table[None] // pages == src[:, None, None])
    rank = jnp.cumsum(owned.astype(jnp.int32), axis=-1) - 1
    pick = owned[:, :, None, :] & (
        rank[:, :, None, :] == jnp.arange(SLOTS, dtype=jnp.int32)[None, None, :, None]
    )
    local = jnp.sum(jnp.where(pick[me], (page_table % pages)[:, None, :], 0), axis=-1)
    room = jnp.clip(
        prefix_len[:, None] - jnp.arange(maxp, dtype=jnp.int32)[None] * page, 0, page
    )
    live = jnp.sum(jnp.where(pick, room[None, :, None, :], 0), axis=-1)
    live = lax.dynamic_slice_in_dim(live, me * reqs, reqs, 1)[:, 0]
    sent = jnp.stack([pool_keys[local], pool_values[local]], axis=1)
    got = lax.all_to_all(sent, "seq", split_axis=0, concat_axis=0, tiled=True)
    keys = got[:, 0].transpose(2, 0, 1, 3, 4).reshape(kvh, -1, hd)
    values = got[:, 1].transpose(2, 0, 1, 3, 4).reshape(kvh, -1, hd)
    seen = (jnp.arange(page, dtype=jnp.int32) < live[..., None]).reshape(1, 1, -1)
    q = queries[0].reshape(fresh, kvh, group, hd).transpose(1, 0, 2, 3).reshape(kvh, -1, hd)
    fk = new_keys[0].transpose(1, 0, 2)
    fv = new_values[0].transpose(1, 0, 2)
    row_c = jnp.arange(fresh * group, dtype=jnp.int32) // group
    causal = (jnp.arange(fresh, dtype=jnp.int32)[None, :] <= row_c[:, None])[None]
    s0 = jnp.einsum("jqd,jkd->jqk", q, keys, preferred_element_type=jnp.float32) * scale
    s1 = jnp.einsum("jqd,jkd->jqk", q, fk, preferred_element_type=jnp.float32) * scale
    s0 = jnp.where(seen, s0, -1e30)
    s1 = jnp.where(causal, s1, -1e30)
    m = jnp.maximum(jnp.max(s0, -1, keepdims=True), jnp.max(s1, -1, keepdims=True))
    w0 = jnp.exp(s0 - m)
    w1 = jnp.exp(s1 - m)
    total = jnp.sum(w0, -1, keepdims=True) + jnp.sum(w1, -1, keepdims=True)
    acc = jnp.einsum(
        "jqk,jkd->jqd", w0.astype(jnp.bfloat16), values, preferred_element_type=jnp.float32
    ) + jnp.einsum(
        "jqk,jkd->jqd", w1.astype(jnp.bfloat16), fv, preferred_element_type=jnp.float32
    )
    attn = (acc / total).astype(jnp.bfloat16)
    attn = attn.reshape(kvh, fresh, group, hd).transpose(1, 0, 2, 3).reshape(fresh, heads * hd)
    part = jnp.dot(attn, out_weight, preferred_element_type=jnp.float32).astype(jnp.bfloat16)
    out = lax.psum_scatter(part, "mp", scatter_dimension=1, tiled=True)
    return out[None]


def solution(mesh):
    in_specs = (
        P("seq", None, "mp", None),
        P("seq", None, "mp", None),
        P("seq", None, "mp", None),
        P("seq", "mp", None, None),
        P("seq", "mp", None, None),
        P(),
        P(),
        P("mp", None),
    )
    return jax.shard_map(
        on_device, mesh=mesh, in_specs=in_specs, out_specs=P("seq", None, "mp"), check_vma=False
    )
```

```python
import functools
import math

import jax
import jax.numpy as jnp
from jax import lax
from jax.experimental import pallas as pl
from jax.experimental.pallas import tpu as pltpu
from jax.sharding import PartitionSpec as P

MESH = pl.DeviceIdType.MESH
SLOTS = 2
FLOOR = -1e30


def flipped(index, mask):
    out, bit = index, 1
    while bit <= mask:
        if mask & bit:
            out = out + bit - 2 * bit * ((index // bit) % 2)
        bit *= 2
    return out


def low_bit(r):
    return r & -r


def kernel(
    dims, len_ref, table_ref, q_ref, nk_ref, nv_ref, pk_ref, pv_ref, w_hbm, out_ref,
    wbuf, qs, sendk, sendv, recvk, recvv, probs, peaks, sums, acc, attn, sbuf, rbuf,
    w_sem, ks_sem, kr_sem, vs_sem, vr_sem, rs_sem, rr_sem,
):
    n, n_mp, order, tiles, width = dims
    fresh = q_ref.shape[0]
    pages, kvh, page, hd = pk_ref.shape
    maxp = table_ref.shape[1]
    group = q_ref.shape[1] // hd // kvh
    lanes = group * fresh
    me = lax.axis_index("seq")
    mz = lax.axis_index("mp")
    coef = math.log2(math.e) / math.sqrt(hd)

    def w_copy(pos, t):
        col = pl.multiple_of((flipped(mz, order[pos]) * tiles + t) * width, 128)
        i = pos * tiles + t
        return pltpu.make_async_copy(w_hbm.at[:, pl.ds(col, width)], wbuf.at[i], w_sem.at[i])

    for pos in range(n_mp):
        for t in range(tiles):
            w_copy(pos, t).start()

    steps = []
    bit = 1
    while bit < n_mp:
        steps.append(bit)
        bit *= 2
    barrier = pltpu.get_barrier_semaphore()
    for k in range(1, n):
        pl.semaphore_signal(
            barrier, inc=1, device_id={"seq": lax.rem(me + k, n)}, device_id_type=MESH
        )
    for bit in steps:
        pl.semaphore_signal(
            barrier, inc=1, device_id={"mp": flipped(mz, bit)}, device_id_type=MESH
        )
    pl.semaphore_wait(barrier, n - 1 + len(steps))

    def scan(row, owner):
        first, count = owner * pages, 0
        ids = [0] * SLOTS
        live = [0] * SLOTS
        length = len_ref[row]
        for l in range(maxp):
            p = table_ref[row, l]
            owned = (p >= first) & (p < first + pages)
            room = jnp.clip(length - l * page, 0, page)
            for s in range(SLOTS):
                here = owned & (count == s)
                ids[s] = jnp.where(here, p - first, ids[s])
                live[s] = jnp.where(here, room, live[s])
            count = count + owned.astype(jnp.int32)
        return ids, live

    def page_copy(send, recv, s_sem, r_sem, k, slot, target):
        return pltpu.make_async_remote_copy(
            src_ref=send.at[k], dst_ref=recv.at[slot], send_sem=s_sem.at[k],
            recv_sem=r_sem.at[slot], device_id={"seq": target}, device_id_type=MESH,
        )

    def send_all(pool, send, recv, s_sem, r_sem):
        def one(k, _):
            target = lax.rem(me + k, n)
            ids, _ = scan(target, me)
            for s in range(SLOTS):
                for j in range(kvh):
                    send[k, j, s] = pool[ids[s], j]
            page_copy(send, recv, s_sem, r_sem, k, me, target).start()
            return 0

        lax.fori_loop(1, n, one, 0)
        ids, _ = scan(me, me)
        for s in range(SLOTS):
            for j in range(kvh):
                recv[me, j, s] = pool[ids[s], j]

    send_all(pk_ref, sendk, recvk, ks_sem, kr_sem)
    send_all(pv_ref, sendv, recvv, vs_sem, vr_sem)

    for h in range(kvh * group):
        j, g = h // group, h % group
        qs[j, g * fresh:(g + 1) * fresh, :] = q_ref[:, h * hd:(h + 1) * hd]

    def scores(keys, j):
        return lax.dot_general(
            keys, qs[j], (((1,), (1,)), ((), ())), preferred_element_type=jnp.float32
        )

    def mixed(values, weights):
        return lax.dot_general(
            values, weights, (((0,), (0,)), ((), ())), preferred_element_type=jnp.float32
        )

    lane = lax.broadcasted_iota(jnp.int32, (fresh, lanes), 1)
    token = lane
    for g in range(1, group):
        token = token - jnp.where(lane >= g * fresh, fresh, 0)
    causal = lax.broadcasted_iota(jnp.int32, (fresh, lanes), 0) <= token
    for j in range(kvh):
        s = jnp.where(causal, scores(nk_ref[:, j * hd:(j + 1) * hd], j), FLOOR)
        m = jnp.max(s, axis=0, keepdims=True)
        w = jnp.exp2((s - m) * coef)
        peaks[n, j] = m
        sums[n, j] = jnp.sum(w, axis=0, keepdims=True)
        acc[j] = mixed(nv_ref[:, j * hd:(j + 1) * hd], w.astype(jnp.bfloat16))

    def score_block(k, _):
        src = lax.rem(me + n - k, n)

        @pl.when(k > 0)
        def _():
            page_copy(sendk, recvk, ks_sem, kr_sem, k, src, src).wait_recv()

        _, live = scan(me, src)
        row = lax.broadcasted_iota(jnp.int32, (SLOTS * page, lanes), 0)
        allowed = row < live[0]
        for s in range(1, SLOTS):
            allowed = allowed | ((row >= s * page) & (row < s * page + live[s]))
        for j in range(kvh):
            s = scores(recvk[src, j].reshape(SLOTS * page, hd), j)
            s = jnp.where(allowed, s, FLOOR)
            m = jnp.max(s, axis=0, keepdims=True)
            w = jnp.exp2((s - m) * coef)
            peaks[k, j] = m
            sums[k, j] = jnp.sum(w, axis=0, keepdims=True)
            probs[k, j] = w.astype(jnp.bfloat16)
        return 0

    lax.fori_loop(0, n, score_block, 0)

    tops = []
    for j in range(kvh):
        top = peaks[n, j]
        for k in range(n):
            top = jnp.maximum(top, peaks[k, j])
        total = jnp.zeros_like(top)
        for k in range(n + 1):
            total = total + sums[k, j] * jnp.exp2((peaks[k, j] - top) * coef)
        acc[j] = acc[j] * jnp.exp2((peaks[n, j] - top) * coef)
        sums[n, j] = total
        peaks[n, j] = top

    def value_block(k, _):
        src = lax.rem(me + n - k, n)

        @pl.when(k > 0)
        def _():
            page_copy(sendv, recvv, vs_sem, vr_sem, k, src, src).wait_recv()

        for j in range(kvh):
            part = mixed(recvv[src, j].reshape(SLOTS * page, hd), probs[k, j])
            acc[j] = acc[j] + part * jnp.exp2((peaks[k, j] - peaks[n, j]) * coef)
        return 0

    lax.fori_loop(0, n, value_block, 0)

    for j in range(kvh):
        heads = (acc[j] / sums[n, j]).T.astype(jnp.bfloat16)
        for g in range(group):
            h = j * group + g
            attn[:, h * hd:(h + 1) * hd] = heads[g * fresh:(g + 1) * fresh, :]

    def sum_copy(r, t):
        return pltpu.make_async_remote_copy(
            src_ref=sbuf.at[r, t], dst_ref=rbuf.at[r, t], send_sem=rs_sem.at[r, t],
            recv_sem=rr_sem.at[r, t], device_id={"mp": flipped(mz, low_bit(r))},
            device_id_type=MESH,
        )

    for pos, r in enumerate(order):
        def project(t, _, pos=pos, r=r):
            i = pos * tiles + t
            pltpu.make_async_copy(
                w_hbm.at[:, pl.ds(0, width)], wbuf.at[i], w_sem.at[i]
            ).wait()
            part = jnp.dot(attn[...], wbuf[i], preferred_element_type=jnp.float32)
            if r:
                for bit in steps:
                    if bit < low_bit(r):
                        sum_copy(r + bit, t).wait_recv()
                        part = part + rbuf[r + bit, t].astype(jnp.float32)
            sbuf[r, t] = part.astype(jnp.bfloat16)
            if r:
                sum_copy(r, t).start()
            return 0

        lax.fori_loop(0, tiles, project, 0)

    for t in range(tiles):
        part = sbuf[0, t].astype(jnp.float32)
        for bit in steps:
            sum_copy(bit, t).wait_recv()
            part = part + rbuf[bit, t].astype(jnp.float32)
        out_ref[:, t * width:(t + 1) * width] = part.astype(out_ref.dtype)

    def drain(k, _):
        target = lax.rem(me + k, n)
        page_copy(sendk, recvk, ks_sem, kr_sem, k, me, target).wait_send()
        page_copy(sendv, recvv, vs_sem, vr_sem, k, me, target).wait_send()
        return 0

    lax.fori_loop(1, n, drain, 0)
    for r in range(1, n_mp):
        for t in range(tiles):
            sum_copy(r, t).wait_send()


def on_device(
    n, n_mp, queries, new_keys, new_values, pool_keys, pool_values, prefix_len, page_table, out_weight
):
    reqs, fresh, heads, hd = queries.shape
    pages, kvh, page, _ = pool_keys.shape
    lanes = heads // kvh * fresh
    depth, model = out_weight.shape
    chunk = model // n_mp
    width = min(512, chunk)
    tiles = chunk // width
    order = sorted(range(n_mp), key=lambda r: (low_bit(r) if r else n_mp, -r))
    bf16, f32 = jnp.bfloat16, jnp.float32
    dma = pltpu.SemaphoreType.DMA
    vmem = pl.BlockSpec(memory_space=pltpu.VMEM)
    smem = pl.BlockSpec(memory_space=pltpu.SMEM)
    pages_shape = (n, kvh, SLOTS, page, hd)
    out = pl.pallas_call(
        functools.partial(kernel, (n, n_mp, tuple(order), tiles, width)),
        out_shape=jax.ShapeDtypeStruct((fresh, chunk), bf16),
        in_specs=[smem, smem] + [vmem] * 5 + [pl.BlockSpec(memory_space=pl.ANY)],
        out_specs=vmem,
        scratch_shapes=[
            pltpu.VMEM((n_mp * tiles, depth, width), bf16),
            pltpu.VMEM((kvh, lanes, hd), bf16),
            pltpu.VMEM(pages_shape, bf16),
            pltpu.VMEM(pages_shape, bf16),
            pltpu.VMEM(pages_shape, bf16),
            pltpu.VMEM(pages_shape, bf16),
            pltpu.VMEM((n, kvh, SLOTS * page, lanes), bf16),
            pltpu.VMEM((n + 1, kvh, 1, lanes), f32),
            pltpu.VMEM((n + 1, kvh, 1, lanes), f32),
            pltpu.VMEM((kvh, hd, lanes), f32),
            pltpu.VMEM((fresh, depth), bf16),
            pltpu.VMEM((n_mp, tiles, fresh, width), bf16),
            pltpu.VMEM((n_mp, tiles, fresh, width), bf16),
            dma((n_mp * tiles,)),
            dma((n,)), dma((n,)), dma((n,)), dma((n,)),
            dma((n_mp, tiles)), dma((n_mp, tiles)),
        ],
        compiler_params=pltpu.CompilerParams(
            collective_id=0, has_side_effects=True, vmem_limit_bytes=60 * 2**20
        ),
    )(
        prefix_len,
        page_table,
        queries.reshape(fresh, heads * hd),
        new_keys.reshape(fresh, kvh * hd),
        new_values.reshape(fresh, kvh * hd),
        pool_keys,
        pool_values,
        out_weight,
    )
    return out[None]


def solution(mesh):
    in_specs = (
        P("seq", None, "mp", None),
        P("seq", None, "mp", None),
        P("seq", None, "mp", None),
        P("seq", "mp", None, None),
        P("seq", "mp", None, None),
        P(),
        P(),
        P("mp", None),
    )
    body = functools.partial(on_device, mesh.shape["seq"], mesh.shape["mp"])
    return jax.shard_map(
        body, mesh=mesh, in_specs=in_specs, out_specs=P("seq", None, "mp"), check_vma=False
    )
```

```python
import functools
import math

import jax
import jax.numpy as jnp
from jax import lax
from jax.experimental import pallas as pl
from jax.experimental.pallas import tpu as pltpu
from jax.sharding import PartitionSpec as P

MESH = pl.DeviceIdType.MESH
SLOTS = 2
FLOOR = -1e30


def flipped(index, mask):
    out, bit = index, 1
    while bit <= mask:
        if mask & bit:
            out = out + bit - 2 * bit * ((index // bit) % 2)
        bit *= 2
    return out


def low_bit(r):
    return r & -r


def kernel(
    dims, len_ref, table_ref, q_ref, nk_ref, nv_ref, pk_ref, pv_ref, w_hbm, out_ref,
    wbuf, q32, n32, qs, sendk, sendv, recvk, recvv, probs, peaks, sums, acc, attn, sbuf, rbuf,
    w_sem, ks_sem, kr_sem, vs_sem, vr_sem, rs_sem, rr_sem,
):
    n, n_mp, order, tiles, width = dims
    fresh = q_ref.shape[1]
    pages, kvh, page, hd = pk_ref.shape
    maxp = table_ref.shape[1]
    group = q_ref.shape[2] // kvh
    lanes = group * fresh
    me = lax.axis_index("seq")
    mz = lax.axis_index("mp")
    coef = math.log2(math.e) / math.sqrt(hd)

    def w_copy(pos, t):
        col = pl.multiple_of((flipped(mz, order[pos]) * tiles + t) * width, 128)
        i = pos * tiles + t
        return pltpu.make_async_copy(w_hbm.at[:, pl.ds(col, width)], wbuf.at[i], w_sem.at[i])

    for pos in range(n_mp):
        for t in range(tiles):
            w_copy(pos, t).start()

    steps = []
    bit = 1
    while bit < n_mp:
        steps.append(bit)
        bit *= 2
    barrier = pltpu.get_barrier_semaphore()
    for k in range(1, n):
        pl.semaphore_signal(
            barrier, inc=1, device_id={"seq": lax.rem(me + k, n)}, device_id_type=MESH
        )
    for bit in steps:
        pl.semaphore_signal(
            barrier, inc=1, device_id={"mp": flipped(mz, bit)}, device_id_type=MESH
        )
    pl.semaphore_wait(barrier, n - 1 + len(steps))

    def scan(row, owner):
        first, count = owner * pages, 0
        ids = [0] * SLOTS
        live = [0] * SLOTS
        length = len_ref[row]
        for l in range(maxp):
            p = table_ref[row, l]
            owned = (p >= first) & (p < first + pages)
            room = jnp.clip(length - l * page, 0, page)
            for s in range(SLOTS):
                here = owned & (count == s)
                ids[s] = jnp.where(here, p - first, ids[s])
                live[s] = jnp.where(here, room, live[s])
            count = count + owned.astype(jnp.int32)
        return ids, live

    def page_copy(send, recv, s_sem, r_sem, k, slot, target):
        return pltpu.make_async_remote_copy(
            src_ref=send.at[k], dst_ref=recv.at[slot], send_sem=s_sem.at[k],
            recv_sem=r_sem.at[slot], device_id={"seq": target}, device_id_type=MESH,
        )

    def send_all(pool, send, recv, start):
        def one(k, _):
            target = lax.rem(me + k, n)
            ids, _ = scan(target, me)
            for s in range(SLOTS):
                for j in range(kvh):
                    send[k, j, s] = pool[ids[s], j]
            if start:
                page_copy(send, recv, ks_sem, kr_sem, k, me, target).start()
            return 0

        lax.fori_loop(1, n, one, 0)
        ids, _ = scan(me, me)
        for s in range(SLOTS):
            for j in range(kvh):
                recv[me, j, s] = pool[ids[s], j]

    send_all(pk_ref, sendk, recvk, True)
    send_all(pv_ref, sendv, recvv, False)

    q32[...] = q_ref[0].astype(jnp.float32)
    n32[0] = nk_ref[0].astype(jnp.float32)
    n32[1] = nv_ref[0].astype(jnp.float32)
    for h in range(kvh * group):
        j, g = h // group, h % group
        qs[j, g * fresh:(g + 1) * fresh, :] = q32[:, h, :].astype(jnp.bfloat16)

    def scores(keys, j):
        return lax.dot_general(
            keys, qs[j], (((1,), (1,)), ((), ())), preferred_element_type=jnp.float32
        )

    def mixed(values, weights):
        return lax.dot_general(
            values, weights, (((0,), (0,)), ((), ())), preferred_element_type=jnp.float32
        )

    lane = lax.broadcasted_iota(jnp.int32, (fresh, lanes), 1)
    token = lane
    for g in range(1, group):
        token = token - jnp.where(lane >= g * fresh, fresh, 0)
    causal = lax.broadcasted_iota(jnp.int32, (fresh, lanes), 0) <= token
    for j in range(kvh):
        s = jnp.where(causal, scores(n32[0, :, j, :].astype(jnp.bfloat16), j), FLOOR)
        m = jnp.max(s, axis=0, keepdims=True)
        w = jnp.exp2((s - m) * coef)
        peaks[n, j] = m
        sums[n, j] = jnp.sum(w, axis=0, keepdims=True)
        acc[j] = mixed(n32[1, :, j, :].astype(jnp.bfloat16), w.astype(jnp.bfloat16))

    def send_values(k, _):
        target = lax.rem(me + k, n)
        page_copy(sendk, recvk, ks_sem, kr_sem, k, me, target).wait_send()
        page_copy(sendv, recvv, vs_sem, vr_sem, k, me, target).start()
        return 0

    lax.fori_loop(1, n, send_values, 0)

    def score_block(k, _):
        src = lax.rem(me + n - k, n)

        @pl.when(k > 0)
        def _():
            page_copy(sendk, recvk, ks_sem, kr_sem, k, src, src).wait_recv()

        _, live = scan(me, src)
        row = lax.broadcasted_iota(jnp.int32, (SLOTS * page, lanes), 0)
        allowed = row < live[0]
        for s in range(1, SLOTS):
            allowed = allowed | ((row >= s * page) & (row < s * page + live[s]))
        for j in range(kvh):
            s = scores(recvk[src, j].reshape(SLOTS * page, hd), j)
            s = jnp.where(allowed, s, FLOOR)
            m = jnp.max(s, axis=0, keepdims=True)
            w = jnp.exp2((s - m) * coef)
            peaks[k, j] = m
            sums[k, j] = jnp.sum(w, axis=0, keepdims=True)
            probs[k, j] = w.astype(jnp.bfloat16)
        return 0

    lax.fori_loop(0, n, score_block, 0)

    tops = []
    for j in range(kvh):
        top = peaks[n, j]
        for k in range(n):
            top = jnp.maximum(top, peaks[k, j])
        total = jnp.zeros_like(top)
        for k in range(n + 1):
            total = total + sums[k, j] * jnp.exp2((peaks[k, j] - top) * coef)
        acc[j] = acc[j] * jnp.exp2((peaks[n, j] - top) * coef)
        sums[n, j] = total
        peaks[n, j] = top

    def value_block(k, _):
        src = lax.rem(me + n - k, n)

        @pl.when(k > 0)
        def _():
            page_copy(sendv, recvv, vs_sem, vr_sem, k, src, src).wait_recv()

        for j in range(kvh):
            part = mixed(recvv[src, j].reshape(SLOTS * page, hd), probs[k, j])
            acc[j] = acc[j] + part * jnp.exp2((peaks[k, j] - peaks[n, j]) * coef)
        return 0

    lax.fori_loop(0, n, value_block, 0)

    for j in range(kvh):
        heads = (acc[j] / sums[n, j]).T.astype(jnp.bfloat16)
        for g in range(group):
            h = j * group + g
            attn[:, h * hd:(h + 1) * hd] = heads[g * fresh:(g + 1) * fresh, :]

    def sum_copy(r, t):
        return pltpu.make_async_remote_copy(
            src_ref=sbuf.at[r, t], dst_ref=rbuf.at[r, t], send_sem=rs_sem.at[r, t],
            recv_sem=rr_sem.at[r, t], device_id={"mp": flipped(mz, low_bit(r))},
            device_id_type=MESH,
        )

    for pos, r in enumerate(order):
        def project(t, _, pos=pos, r=r):
            i = pos * tiles + t
            pltpu.make_async_copy(
                w_hbm.at[:, pl.ds(0, width)], wbuf.at[i], w_sem.at[i]
            ).wait()
            part = jnp.dot(attn[...], wbuf[i], preferred_element_type=jnp.float32)
            if r:
                for bit in steps:
                    if bit < low_bit(r):
                        sum_copy(r + bit, t).wait_recv()
                        part = part + rbuf[r + bit, t].astype(jnp.float32)
            sbuf[r, t] = part.astype(jnp.bfloat16)
            if r:
                sum_copy(r, t).start()
            return 0

        lax.fori_loop(0, tiles, project, 0)

    for t in range(tiles):
        part = sbuf[0, t].astype(jnp.float32)
        for bit in steps:
            sum_copy(bit, t).wait_recv()
            part = part + rbuf[bit, t].astype(jnp.float32)
        out_ref[:, t * width:(t + 1) * width] = part.astype(out_ref.dtype)

    def drain(k, _):
        target = lax.rem(me + k, n)
        page_copy(sendv, recvv, vs_sem, vr_sem, k, me, target).wait_send()
        return 0

    lax.fori_loop(1, n, drain, 0)
    for r in range(1, n_mp):
        for t in range(tiles):
            sum_copy(r, t).wait_send()


def on_device(
    n, n_mp, queries, new_keys, new_values, pool_keys, pool_values, prefix_len, page_table, out_weight
):
    reqs, fresh, heads, hd = queries.shape
    pages, kvh, page, _ = pool_keys.shape
    lanes = heads // kvh * fresh
    depth, model = out_weight.shape
    chunk = model // n_mp
    width = min(512, chunk)
    tiles = chunk // width
    order = sorted(range(n_mp), key=lambda r: (low_bit(r) if r else n_mp, -r))
    bf16, f32 = jnp.bfloat16, jnp.float32
    dma = pltpu.SemaphoreType.DMA
    vmem = pl.BlockSpec(memory_space=pltpu.VMEM)
    smem = pl.BlockSpec(memory_space=pltpu.SMEM)
    pages_shape = (n, kvh, SLOTS, page, hd)
    out = pl.pallas_call(
        functools.partial(kernel, (n, n_mp, tuple(order), tiles, width)),
        out_shape=jax.ShapeDtypeStruct((fresh, chunk), bf16),
        in_specs=[smem, smem] + [vmem] * 5 + [pl.BlockSpec(memory_space=pl.ANY)],
        out_specs=vmem,
        scratch_shapes=[
            pltpu.VMEM((n_mp * tiles, depth, width), bf16),
            pltpu.VMEM((fresh, heads, hd), f32),
            pltpu.VMEM((2, fresh, kvh, hd), f32),
            pltpu.VMEM((kvh, lanes, hd), bf16),
            pltpu.VMEM(pages_shape, bf16),
            pltpu.VMEM(pages_shape, bf16),
            pltpu.VMEM(pages_shape, bf16),
            pltpu.VMEM(pages_shape, bf16),
            pltpu.VMEM((n, kvh, SLOTS * page, lanes), bf16),
            pltpu.VMEM((n + 1, kvh, 1, lanes), f32),
            pltpu.VMEM((n + 1, kvh, 1, lanes), f32),
            pltpu.VMEM((kvh, hd, lanes), f32),
            pltpu.VMEM((fresh, depth), bf16),
            pltpu.VMEM((n_mp, tiles, fresh, width), bf16),
            pltpu.VMEM((n_mp, tiles, fresh, width), bf16),
            dma((n_mp * tiles,)),
            dma((n,)), dma((n,)), dma((n,)), dma((n,)),
            dma((n_mp, tiles)), dma((n_mp, tiles)),
        ],
        compiler_params=pltpu.CompilerParams(
            collective_id=0, has_side_effects=True, vmem_limit_bytes=60 * 2**20
        ),
    )(
        prefix_len,
        page_table,
        queries,
        new_keys,
        new_values,
        pool_keys,
        pool_values,
        out_weight,
    )
    return out[None]


def solution(mesh):
    in_specs = (
        P("seq", None, "mp", None),
        P("seq", None, "mp", None),
        P("seq", None, "mp", None),
        P("seq", "mp", None, None),
        P("seq", "mp", None, None),
        P(),
        P(),
        P("mp", None),
    )
    body = functools.partial(on_device, mesh.shape["seq"], mesh.shape["mp"])
    return jax.shard_map(
        body, mesh=mesh, in_specs=in_specs, out_specs=P("seq", None, "mp"), check_vma=False
    )
```

```python
import functools
import math

import jax
import jax.numpy as jnp
from jax import lax
from jax.experimental import pallas as pl
from jax.experimental.pallas import tpu as pltpu
from jax.sharding import PartitionSpec as P

MESH = pl.DeviceIdType.MESH
SLOTS = 2
FLOOR = -1e30


def flipped(index, mask):
    out, bit = index, 1
    while bit <= mask:
        if mask & bit:
            out = out + bit - 2 * bit * ((index // bit) % 2)
        bit *= 2
    return out


def low_bit(r):
    return r & -r


def kernel(
    dims, len_ref, table_ref, nk_ref, nv_ref, q_hbm, pk_hbm, pv_hbm, w_hbm, out_ref,
    pk_ref, pv_ref, q_ref, wbuf, q32, n32, qs, sendk, sendv, recvk, recvv, probs, peaks, sums, acc, attn, sbuf, rbuf,
    in_sem, w_sem, ks_sem, kr_sem, vs_sem, vr_sem, rs_sem, rr_sem,
):
    n, n_mp, order, tiles, width = dims
    fresh = q_ref.shape[1]
    pages, kvh, page, hd = pk_ref.shape
    maxp = table_ref.shape[1]
    group = q_ref.shape[2] // kvh
    lanes = group * fresh
    me = lax.axis_index("seq")
    mz = lax.axis_index("mp")
    coef = math.log2(math.e) / math.sqrt(hd)

    loads = [
        pltpu.make_async_copy(src, dst, in_sem.at[i])
        for i, (src, dst) in enumerate(((pk_hbm, pk_ref), (pv_hbm, pv_ref), (q_hbm, q_ref)))
    ]

    def w_copy(pos, t):
        col = pl.multiple_of((flipped(mz, order[pos]) * tiles + t) * width, 128)
        i = pos * tiles + t
        return pltpu.make_async_copy(w_hbm.at[:, pl.ds(col, width)], wbuf.at[i], w_sem.at[i])

    steps = []
    bit = 1
    while bit < n_mp:
        steps.append(bit)
        bit *= 2
    barrier = pltpu.get_barrier_semaphore()
    for k in range(1, n):
        pl.semaphore_signal(
            barrier, inc=1, device_id={"seq": lax.rem(me + k, n)}, device_id_type=MESH
        )
    for bit in steps:
        pl.semaphore_signal(
            barrier, inc=1, device_id={"mp": flipped(mz, bit)}, device_id_type=MESH
        )
    for load in loads:
        load.start()
    pl.semaphore_wait(barrier, n - 1 + len(steps))

    def scan(row, owner):
        first, count = owner * pages, 0
        ids = [0] * SLOTS
        live = [0] * SLOTS
        length = len_ref[row]
        for l in range(maxp):
            p = table_ref[row, l]
            owned = (p >= first) & (p < first + pages)
            room = jnp.clip(length - l * page, 0, page)
            for s in range(SLOTS):
                here = owned & (count == s)
                ids[s] = jnp.where(here, p - first, ids[s])
                live[s] = jnp.where(here, room, live[s])
            count = count + owned.astype(jnp.int32)
        return ids, live

    def page_copy(send, recv, s_sem, r_sem, k, slot, target):
        return pltpu.make_async_remote_copy(
            src_ref=send.at[k], dst_ref=recv.at[slot], send_sem=s_sem.at[k],
            recv_sem=r_sem.at[slot], device_id={"seq": target}, device_id_type=MESH,
        )

    def send_all(pool, send, recv, start):
        def one(k, _):
            target = lax.rem(me + k, n)
            ids, _ = scan(target, me)
            for s in range(SLOTS):
                for j in range(kvh):
                    send[k, j, s] = pool[ids[s], j]
            if start:
                page_copy(send, recv, ks_sem, kr_sem, k, me, target).start()
            return 0

        lax.fori_loop(1, n, one, 0)
        ids, _ = scan(me, me)
        for s in range(SLOTS):
            for j in range(kvh):
                recv[me, j, s] = pool[ids[s], j]

    loads[0].wait()
    send_all(pk_ref, sendk, recvk, True)
    loads[1].wait()
    send_all(pv_ref, sendv, recvv, False)
    loads[2].wait()
    for pos in range(n_mp):
        for t in range(tiles):
            w_copy(pos, t).start()

    q32[...] = q_ref[0].astype(jnp.float32)
    n32[0] = nk_ref[0].astype(jnp.float32)
    n32[1] = nv_ref[0].astype(jnp.float32)
    for h in range(kvh * group):
        j, g = h // group, h % group
        qs[j, g * fresh:(g + 1) * fresh, :] = q32[:, h, :].astype(jnp.bfloat16)

    def scores(keys, j):
        return lax.dot_general(
            keys, qs[j], (((1,), (1,)), ((), ())), preferred_element_type=jnp.float32
        )

    def mixed(values, weights):
        return lax.dot_general(
            values, weights, (((0,), (0,)), ((), ())), preferred_element_type=jnp.float32
        )

    lane = lax.broadcasted_iota(jnp.int32, (fresh, lanes), 1)
    token = lane
    for g in range(1, group):
        token = token - jnp.where(lane >= g * fresh, fresh, 0)
    causal = lax.broadcasted_iota(jnp.int32, (fresh, lanes), 0) <= token
    for j in range(kvh):
        s = jnp.where(causal, scores(n32[0, :, j, :].astype(jnp.bfloat16), j), FLOOR)
        m = jnp.max(s, axis=0, keepdims=True)
        w = jnp.exp2((s - m) * coef)
        peaks[n, j] = m
        sums[n, j] = jnp.sum(w, axis=0, keepdims=True)
        acc[j] = mixed(n32[1, :, j, :].astype(jnp.bfloat16), w.astype(jnp.bfloat16))

    def send_values(k, _):
        target = lax.rem(me + k, n)
        page_copy(sendk, recvk, ks_sem, kr_sem, k, me, target).wait_send()
        page_copy(sendv, recvv, vs_sem, vr_sem, k, me, target).start()
        return 0

    lax.fori_loop(1, n, send_values, 0)

    def score_block(k, _):
        src = lax.rem(me + n - k, n)

        @pl.when(k > 0)
        def _():
            page_copy(sendk, recvk, ks_sem, kr_sem, k, src, src).wait_recv()

        _, live = scan(me, src)
        row = lax.broadcasted_iota(jnp.int32, (SLOTS * page, lanes), 0)
        allowed = row < live[0]
        for s in range(1, SLOTS):
            allowed = allowed | ((row >= s * page) & (row < s * page + live[s]))
        for j in range(kvh):
            s = scores(recvk[src, j].reshape(SLOTS * page, hd), j)
            s = jnp.where(allowed, s, FLOOR)
            m = jnp.max(s, axis=0, keepdims=True)
            w = jnp.exp2((s - m) * coef)
            peaks[k, j] = m
            sums[k, j] = jnp.sum(w, axis=0, keepdims=True)
            probs[k, j] = w.astype(jnp.bfloat16)
        return 0

    lax.fori_loop(0, n, score_block, 0)

    tops = []
    for j in range(kvh):
        top = peaks[n, j]
        for k in range(n):
            top = jnp.maximum(top, peaks[k, j])
        total = jnp.zeros_like(top)
        for k in range(n + 1):
            total = total + sums[k, j] * jnp.exp2((peaks[k, j] - top) * coef)
        acc[j] = acc[j] * jnp.exp2((peaks[n, j] - top) * coef)
        sums[n, j] = total
        peaks[n, j] = top

    def value_block(k, _):
        src = lax.rem(me + n - k, n)

        @pl.when(k > 0)
        def _():
            page_copy(sendv, recvv, vs_sem, vr_sem, k, src, src).wait_recv()

        for j in range(kvh):
            part = mixed(recvv[src, j].reshape(SLOTS * page, hd), probs[k, j])
            acc[j] = acc[j] + part * jnp.exp2((peaks[k, j] - peaks[n, j]) * coef)
        return 0

    lax.fori_loop(0, n, value_block, 0)

    for j in range(kvh):
        heads = (acc[j] / sums[n, j]).T.astype(jnp.bfloat16)
        for g in range(group):
            h = j * group + g
            attn[:, h * hd:(h + 1) * hd] = heads[g * fresh:(g + 1) * fresh, :]

    def sum_copy(r, t):
        return pltpu.make_async_remote_copy(
            src_ref=sbuf.at[r, t], dst_ref=rbuf.at[r, t], send_sem=rs_sem.at[r, t],
            recv_sem=rr_sem.at[r, t], device_id={"mp": flipped(mz, low_bit(r))},
            device_id_type=MESH,
        )

    for pos, r in enumerate(order):
        def project(t, _, pos=pos, r=r):
            i = pos * tiles + t
            pltpu.make_async_copy(
                w_hbm.at[:, pl.ds(0, width)], wbuf.at[i], w_sem.at[i]
            ).wait()
            part = jnp.dot(attn[...], wbuf[i], preferred_element_type=jnp.float32)
            if r:
                for bit in steps:
                    if bit < low_bit(r):
                        sum_copy(r + bit, t).wait_recv()
                        part = part + rbuf[r + bit, t].astype(jnp.float32)
            sbuf[r, t] = part.astype(jnp.bfloat16)
            if r:
                sum_copy(r, t).start()
            return 0

        lax.fori_loop(0, tiles, project, 0)

    for t in range(tiles):
        part = sbuf[0, t].astype(jnp.float32)
        for bit in steps:
            sum_copy(bit, t).wait_recv()
            part = part + rbuf[bit, t].astype(jnp.float32)
        out_ref[:, t * width:(t + 1) * width] = part.astype(out_ref.dtype)

    def drain(k, _):
        target = lax.rem(me + k, n)
        page_copy(sendv, recvv, vs_sem, vr_sem, k, me, target).wait_send()
        return 0

    lax.fori_loop(1, n, drain, 0)
    for r in range(1, n_mp):
        for t in range(tiles):
            sum_copy(r, t).wait_send()


def on_device(
    n, n_mp, queries, new_keys, new_values, pool_keys, pool_values, prefix_len, page_table, out_weight
):
    reqs, fresh, heads, hd = queries.shape
    pages, kvh, page, _ = pool_keys.shape
    lanes = heads // kvh * fresh
    depth, model = out_weight.shape
    chunk = model // n_mp
    width = min(512, chunk)
    tiles = chunk // width
    order = sorted(range(n_mp), key=lambda r: (low_bit(r) if r else n_mp, -r))
    bf16, f32 = jnp.bfloat16, jnp.float32
    dma = pltpu.SemaphoreType.DMA
    vmem = pl.BlockSpec(memory_space=pltpu.VMEM)
    smem = pl.BlockSpec(memory_space=pltpu.SMEM)
    pages_shape = (n, kvh, SLOTS, page, hd)
    out = pl.pallas_call(
        functools.partial(kernel, (n, n_mp, tuple(order), tiles, width)),
        out_shape=jax.ShapeDtypeStruct((fresh, chunk), bf16),
        in_specs=[smem, smem, vmem, vmem] + [pl.BlockSpec(memory_space=pl.ANY)] * 4,
        out_specs=vmem,
        scratch_shapes=[
            pltpu.VMEM(pool_keys.shape, bf16),
            pltpu.VMEM(pool_values.shape, bf16),
            pltpu.VMEM(queries.shape, bf16),
            pltpu.VMEM((n_mp * tiles, depth, width), bf16),
            pltpu.VMEM((fresh, heads, hd), f32),
            pltpu.VMEM((2, fresh, kvh, hd), f32),
            pltpu.VMEM((kvh, lanes, hd), bf16),
            pltpu.VMEM(pages_shape, bf16),
            pltpu.VMEM(pages_shape, bf16),
            pltpu.VMEM(pages_shape, bf16),
            pltpu.VMEM(pages_shape, bf16),
            pltpu.VMEM((n, kvh, SLOTS * page, lanes), bf16),
            pltpu.VMEM((n + 1, kvh, 1, lanes), f32),
            pltpu.VMEM((n + 1, kvh, 1, lanes), f32),
            pltpu.VMEM((kvh, hd, lanes), f32),
            pltpu.VMEM((fresh, depth), bf16),
            pltpu.VMEM((n_mp, tiles, fresh, width), bf16),
            pltpu.VMEM((n_mp, tiles, fresh, width), bf16),
            dma((3,)),
            dma((n_mp * tiles,)),
            dma((n,)), dma((n,)), dma((n,)), dma((n,)),
            dma((n_mp, tiles)), dma((n_mp, tiles)),
        ],
        compiler_params=pltpu.CompilerParams(
            collective_id=0, has_side_effects=True, vmem_limit_bytes=60 * 2**20
        ),
    )(
        prefix_len,
        page_table,
        new_keys,
        new_values,
        queries,
        pool_keys,
        pool_values,
        out_weight,
    )
    return out[None]


def solution(mesh):
    in_specs = (
        P("seq", None, "mp", None),
        P("seq", None, "mp", None),
        P("seq", None, "mp", None),
        P("seq", "mp", None, None),
        P("seq", "mp", None, None),
        P(),
        P(),
        P("mp", None),
    )
    body = functools.partial(on_device, mesh.shape["seq"], mesh.shape["mp"])
    return jax.shard_map(
        body, mesh=mesh, in_specs=in_specs, out_specs=P("seq", None, "mp"), check_vma=False
    )
```

```python
import functools
import math

import jax
import jax.numpy as jnp
from jax import lax
from jax.experimental import pallas as pl
from jax.experimental.pallas import tpu as pltpu
from jax.sharding import PartitionSpec as P

MESH = pl.DeviceIdType.MESH
SLOTS = 2
FLOOR = -1e30


def flipped(index, mask):
    out, bit = index, 1
    while bit <= mask:
        if mask & bit:
            out = out + bit - 2 * bit * ((index // bit) % 2)
        bit *= 2
    return out


def low_bit(r):
    return r & -r


def kernel(
    dims, len_ref, table_ref, nk_ref, nv_ref, q_hbm, pk_hbm, pv_hbm, w_hbm, out_ref,
    pk_ref, pv_ref, q_ref, wbuf, q32, n32, qs, sendk, sendv, recvk, recvv, probs, peaks, sums, acc, attn, sbuf, rbuf,
    in_sem, w_sem, ks_sem, kr_sem, vs_sem, vr_sem, rs_sem, rr_sem,
):
    n, n_mp, order, tiles, width = dims
    fresh = q_ref.shape[1]
    pages, kvh, page, hd = pk_ref.shape
    maxp = table_ref.shape[1]
    group = q_ref.shape[2] // kvh
    lanes = group * fresh
    me = lax.axis_index("seq")
    mz = lax.axis_index("mp")
    coef = math.log2(math.e) / math.sqrt(hd)

    loads = [
        pltpu.make_async_copy(src, dst, in_sem.at[i])
        for i, (src, dst) in enumerate(((pk_hbm, pk_ref), (pv_hbm, pv_ref), (q_hbm, q_ref)))
    ]

    def w_copy(pos, t):
        col = pl.multiple_of((flipped(mz, order[pos]) * tiles + t) * width, 128)
        i = pos * tiles + t
        return pltpu.make_async_copy(w_hbm.at[:, pl.ds(col, width)], wbuf.at[i], w_sem.at[i])

    steps = []
    bit = 1
    while bit < n_mp:
        steps.append(bit)
        bit *= 2
    barrier = pltpu.get_barrier_semaphore()
    for k in range(1, n):
        pl.semaphore_signal(
            barrier, inc=1, device_id={"seq": lax.rem(me + k, n)}, device_id_type=MESH
        )
    for bit in steps:
        pl.semaphore_signal(
            barrier, inc=1, device_id={"mp": flipped(mz, bit)}, device_id_type=MESH
        )
    for load in loads:
        load.start()
    pl.semaphore_wait(barrier, n - 1 + len(steps))

    def scan(row, owner):
        first, count = owner * pages, 0
        ids = [0] * SLOTS
        live = [0] * SLOTS
        length = len_ref[row]
        for l in range(maxp):
            p = table_ref[row, l]
            owned = (p >= first) & (p < first + pages)
            room = jnp.clip(length - l * page, 0, page)
            for s in range(SLOTS):
                here = owned & (count == s)
                ids[s] = jnp.where(here, p - first, ids[s])
                live[s] = jnp.where(here, room, live[s])
            count = count + owned.astype(jnp.int32)
        return ids, live

    def page_copy(send, recv, s_sem, r_sem, k, slot, target):
        return pltpu.make_async_remote_copy(
            src_ref=send.at[k], dst_ref=recv.at[slot], send_sem=s_sem.at[k],
            recv_sem=r_sem.at[slot], device_id={"seq": target}, device_id_type=MESH,
        )

    def send_all(pool, send, recv, start):
        def one(k, _):
            target = lax.rem(me + k, n)
            ids, _ = scan(target, me)
            for s in range(SLOTS):
                for j in range(kvh):
                    send[k, j, s] = pool[ids[s], j]
            if start:
                page_copy(send, recv, ks_sem, kr_sem, k, me, target).start()
            return 0

        lax.fori_loop(1, n, one, 0)
        ids, _ = scan(me, me)
        for s in range(SLOTS):
            for j in range(kvh):
                recv[me, j, s] = pool[ids[s], j]

    loads[0].wait()
    send_all(pk_ref, sendk, recvk, True)
    loads[1].wait()
    send_all(pv_ref, sendv, recvv, False)
    loads[2].wait()
    for pos in range(n_mp):
        for t in range(tiles):
            w_copy(pos, t).start()

    q32[...] = q_ref[0].astype(jnp.float32)
    n32[0] = nk_ref[0].astype(jnp.float32)
    n32[1] = nv_ref[0].astype(jnp.float32)
    for h in range(kvh * group):
        j, g = h // group, h % group
        qs[j, g * fresh:(g + 1) * fresh, :] = q32[:, h, :].astype(jnp.bfloat16)

    def scores(keys, j):
        return lax.dot_general(
            keys, qs[j], (((1,), (1,)), ((), ())), preferred_element_type=jnp.float32
        )

    def mixed(values, weights):
        return lax.dot_general(
            values, weights, (((0,), (0,)), ((), ())), preferred_element_type=jnp.float32
        )

    lane = lax.broadcasted_iota(jnp.int32, (fresh, lanes), 1)
    token = lane
    for g in range(1, group):
        token = token - jnp.where(lane >= g * fresh, fresh, 0)
    causal = lax.broadcasted_iota(jnp.int32, (fresh, lanes), 0) <= token
    for j in range(kvh):
        s = jnp.where(causal, scores(n32[0, :, j, :].astype(jnp.bfloat16), j), FLOOR)
        m = jnp.max(s, axis=0, keepdims=True)
        w = jnp.exp2((s - m) * coef)
        peaks[n, j] = m
        sums[n, j] = jnp.sum(w, axis=0, keepdims=True)
        acc[j] = mixed(n32[1, :, j, :].astype(jnp.bfloat16), w.astype(jnp.bfloat16))

    def send_values(k, _):
        target = lax.rem(me + k, n)
        page_copy(sendk, recvk, ks_sem, kr_sem, k, me, target).wait_send()
        page_copy(sendv, recvv, vs_sem, vr_sem, k, me, target).start()
        return 0

    lax.fori_loop(1, n, send_values, 0)

    def score_block(k, _):
        src = lax.rem(me + n - k, n)

        @pl.when(k > 0)
        def _():
            page_copy(sendk, recvk, ks_sem, kr_sem, k, src, src).wait_recv()

        _, live = scan(me, src)
        row = lax.broadcasted_iota(jnp.int32, (SLOTS * page, lanes), 0)
        allowed = row < live[0]
        for s in range(1, SLOTS):
            allowed = allowed | ((row >= s * page) & (row < s * page + live[s]))
        for j in range(kvh):
            s = scores(recvk[src, j].reshape(SLOTS * page, hd), j)
            s = jnp.where(allowed, s, FLOOR)
            m = jnp.max(s, axis=0, keepdims=True)
            w = jnp.exp2((s - m) * coef)
            peaks[k, j] = m
            sums[k, j] = jnp.sum(w, axis=0, keepdims=True)
            probs[k, j] = w.astype(jnp.bfloat16)
        return 0

    lax.fori_loop(0, n, score_block, 0)

    tops = []
    for j in range(kvh):
        top = peaks[n, j]
        for k in range(n):
            top = jnp.maximum(top, peaks[k, j])
        total = jnp.zeros_like(top)
        for k in range(n + 1):
            total = total + sums[k, j] * jnp.exp2((peaks[k, j] - top) * coef)
        acc[j] = acc[j] * jnp.exp2((peaks[n, j] - top) * coef)
        sums[n, j] = total
        peaks[n, j] = top

    def value_block(k, _):
        src = lax.rem(me + n - k, n)

        @pl.when(k > 0)
        def _():
            page_copy(sendv, recvv, vs_sem, vr_sem, k, src, src).wait_recv()

        for j in range(kvh):
            part = mixed(recvv[src, j].reshape(SLOTS * page, hd), probs[k, j])
            acc[j] = acc[j] + part * jnp.exp2((peaks[k, j] - peaks[n, j]) * coef)
        return 0

    lax.fori_loop(0, n, value_block, 0)

    for j in range(kvh):
        heads = (acc[j] / sums[n, j]).T.astype(jnp.bfloat16)
        for g in range(group):
            h = j * group + g
            attn[:, h * hd:(h + 1) * hd] = heads[g * fresh:(g + 1) * fresh, :]

    def sum_copy(r, t):
        return pltpu.make_async_remote_copy(
            src_ref=sbuf.at[r, t], dst_ref=rbuf.at[r, t], send_sem=rs_sem.at[r, t],
            recv_sem=rr_sem.at[r, t], device_id={"mp": flipped(mz, low_bit(r))},
            device_id_type=MESH,
        )

    for pos, r in enumerate(order):
        def project(t, _, pos=pos, r=r):
            i = pos * tiles + t
            pltpu.make_async_copy(
                w_hbm.at[:, pl.ds(0, width)], wbuf.at[i], w_sem.at[i]
            ).wait()
            part = jnp.dot(attn[...], wbuf[i], preferred_element_type=jnp.float32)
            if r:
                for bit in steps:
                    if bit < low_bit(r):
                        sum_copy(r + bit, t).wait_recv()
                        part = part + rbuf[r + bit, t].astype(jnp.float32)
            sbuf[r, t] = part.astype(jnp.bfloat16)
            if r:
                sum_copy(r, t).start()
            return 0

        lax.fori_loop(0, tiles, project, 0)

    for t in range(tiles):
        part = sbuf[0, t].astype(jnp.float32)
        for bit in steps:
            sum_copy(bit, t).wait_recv()
            part = part + rbuf[bit, t].astype(jnp.float32)
        out_ref[:, t * width:(t + 1) * width] = part.astype(out_ref.dtype)

    def drain(k, _):
        target = lax.rem(me + k, n)
        page_copy(sendv, recvv, vs_sem, vr_sem, k, me, target).wait_send()
        return 0

    lax.fori_loop(1, n, drain, 0)
    for r in range(1, n_mp):
        for t in range(tiles):
            sum_copy(r, t).wait_send()


def on_device(
    n, n_mp, queries, new_keys, new_values, pool_keys, pool_values, prefix_len, page_table, out_weight
):
    reqs, fresh, heads, hd = queries.shape
    pages, kvh, page, _ = pool_keys.shape
    lanes = heads // kvh * fresh
    depth, model = out_weight.shape
    chunk = model // n_mp
    width = min(512, chunk)
    tiles = chunk // width
    order = range(n_mp - 1, -1, -1)
    bf16, f32 = jnp.bfloat16, jnp.float32
    dma = pltpu.SemaphoreType.DMA
    vmem = pl.BlockSpec(memory_space=pltpu.VMEM)
    smem = pl.BlockSpec(memory_space=pltpu.SMEM)
    pages_shape = (n, kvh, SLOTS, page, hd)
    out = pl.pallas_call(
        functools.partial(kernel, (n, n_mp, tuple(order), tiles, width)),
        out_shape=jax.ShapeDtypeStruct((fresh, chunk), bf16),
        in_specs=[smem, smem, vmem, vmem] + [pl.BlockSpec(memory_space=pl.ANY)] * 4,
        out_specs=vmem,
        scratch_shapes=[
            pltpu.VMEM(pool_keys.shape, bf16),
            pltpu.VMEM(pool_values.shape, bf16),
            pltpu.VMEM(queries.shape, bf16),
            pltpu.VMEM((n_mp * tiles, depth, width), bf16),
            pltpu.VMEM((fresh, heads, hd), f32),
            pltpu.VMEM((2, fresh, kvh, hd), f32),
            pltpu.VMEM((kvh, lanes, hd), bf16),
            pltpu.VMEM(pages_shape, bf16),
            pltpu.VMEM(pages_shape, bf16),
            pltpu.VMEM(pages_shape, bf16),
            pltpu.VMEM(pages_shape, bf16),
            pltpu.VMEM((n, kvh, SLOTS * page, lanes), bf16),
            pltpu.VMEM((n + 1, kvh, 1, lanes), f32),
            pltpu.VMEM((n + 1, kvh, 1, lanes), f32),
            pltpu.VMEM((kvh, hd, lanes), f32),
            pltpu.VMEM((fresh, depth), bf16),
            pltpu.VMEM((n_mp, tiles, fresh, width), bf16),
            pltpu.VMEM((n_mp, tiles, fresh, width), bf16),
            dma((3,)),
            dma((n_mp * tiles,)),
            dma((n,)), dma((n,)), dma((n,)), dma((n,)),
            dma((n_mp, tiles)), dma((n_mp, tiles)),
        ],
        compiler_params=pltpu.CompilerParams(
            collective_id=0, has_side_effects=True, vmem_limit_bytes=60 * 2**20
        ),
    )(
        prefix_len,
        page_table,
        new_keys,
        new_values,
        queries,
        pool_keys,
        pool_values,
        out_weight,
    )
    return out[None]


def solution(mesh):
    in_specs = (
        P("seq", None, "mp", None),
        P("seq", None, "mp", None),
        P("seq", None, "mp", None),
        P("seq", "mp", None, None),
        P("seq", "mp", None, None),
        P(),
        P(),
        P("mp", None),
    )
    body = functools.partial(on_device, mesh.shape["seq"], mesh.shape["mp"])
    return jax.shard_map(
        body, mesh=mesh, in_specs=in_specs, out_specs=P("seq", None, "mp"), check_vma=False
    )
```
